32 devices in a mesh: groups: 2 (over y), sub: 4 (over z), gauge: 2 (over x), tm: 2 (over core).
Axes of the slice: x: 2, y: 2, z: 4, core: 2. Of those that a mesh axis runs over, the one named last changes fastest.
Arguments:
- library: float32 [1024, 128, 256], P(('groups', 'sub'), 'gauge'), parts along dimension 0, may hold values from -0.25 to 0.25
- rates: float32 [16, 8, 512], P('groups', 'sub', 'tm'), parts along dimension 0, may hold values from -6 to 6
- subfault_ids: int32 [16, 8], P('groups', 'sub'), parts along dimension 0, may hold values from 0 to 511, as said below
- onsets: int32 [16, 8], P('groups', 'sub'), parts along dimension 0, may hold values from 0 to 511
Outputs:
- wave: float32 [128, 16, 512], P(('gauge', 'sub'), 'groups', 'tm'), parts along dimension 1
The draws below stay inside these ranges and needn't reach their ends.
There are 2 independent parts, one for each index of `groups`. The reference program is written for one: setup_inputs(seed, part) draws one part's arguments, and reference() takes and returns one part's arrays. A program takes and returns all parts, laid end to end along the dimension named above; each array names one. Nothing has to cross between parts.
Inputs may be any that keep to these rules, and one draw needn't show every extreme that they name: `subfault_ids`: owner of an id is id // 128. In each aligned block of 2 columns, at most 12 of its 8 x 2 entries have one owner; one owner is named by exactly 12 entries of every block.
All inputs are finite; a program needn't handle non-finite values.
Results may differ from the reference program's by a relative error of at most 0.0003.
Values sent between devices are 32-bit elements; how exact they have to be, the bound alone decides.
A program may use at most 128 MiB of HBM per device.

```python
import jax
import jax.numpy as jnp
from jax import lax

SCEN = 8
EDEV = 2
FDEV = 128
TAPS = 256
ACTIVE = 8
SUBFAULTS = 512
GAUGES = 128
SAMPLES = 512
CAP = 12


def draw_subfault_ids(key, part):
    block_count = ACTIVE // EDEV
    owner_count = SUBFAULTS // FDEV
    row_width = SCEN * EDEV
    slot_count = owner_count * CAP
    priority = jax.random.permutation(jax.random.fold_in(key, 11), owner_count)
    slot_owner = jnp.arange(slot_count, dtype=jnp.int32) // CAP
    slot_priority = priority[slot_owner]
    hot_flag = (slot_priority == owner_count - 1).astype(jnp.int32)

    def one_block(block_index):
        block_key = jax.random.fold_in(jax.random.fold_in(key, 23), block_index)
        jitter = jax.random.randint(jax.random.fold_in(block_key, 1), (slot_count,), 0, 4096)
        scores = (hot_flag * 1048576 + slot_priority * 256 + jitter) * slot_count + jnp.arange(slot_count, dtype=jnp.int32)
        _, chosen = lax.top_k(scores, row_width)
        shuffle = jax.random.permutation(jax.random.fold_in(block_key, 2), row_width)
        owner_of = chosen[shuffle] // CAP
        local_index = jax.random.randint(jax.random.fold_in(block_key, 3), (row_width,), 0, FDEV)
        return (owner_of * FDEV + local_index).astype(jnp.int32).reshape(SCEN, EDEV)
    blocks_all = jax.vmap(one_block)(jnp.arange(block_count, dtype=jnp.int32))
    return jnp.transpose(blocks_all, (1, 0, 2)).reshape(SCEN, ACTIVE)


def place_ends(entries, stream_key, smallest, largest):
    dims = entries.shape
    place = [jax.random.randint(jax.random.fold_in(stream_key, axis), (), 0, dims[axis]) for axis in range(len(dims))]
    entries = entries.at[tuple(place)].set(smallest)
    longest = dims.index(max(dims))
    place[longest] = (place[longest] + 1) % dims[longest]
    return entries.at[tuple(place)].set(largest)


def spiked(values, rng, source, target, blocks, factor):
    owner, partner = [(jnp.arange(values.shape[position]) // (values.shape[position] // blocks)).reshape([-1 if axis == position else 1 for axis in range(values.ndim)]) for position in (source, target)]
    chosen = jax.random.permutation(rng, blocks)[partner]
    strong = (owner == chosen) | (owner == (partner + blocks // 2) % blocks)
    return jnp.where(strong, factor * values, values)


def block_levels(own_key, extent, shards, smallest, largest):
    factor_of, own = 1.0, jax.random.fold_in(own_key, 6)
    for dim, parts in shards:
        draws = jnp.exp(jax.random.uniform(jax.random.fold_in(own, dim), (parts,), jnp.float32, smallest / len(shards), largest / len(shards)))
        factor_of = factor_of * jnp.repeat(draws, extent[dim] // parts).reshape([-1 if axis == dim else 1 for axis in range(len(extent))])
    return factor_of


def noise(stream_key, dims, width, reach, split=(), held_as=jnp.bfloat16):
    values = jax.random.normal(stream_key, dims, jnp.float32) * width
    if len(split) > 0:
        values = block_levels(stream_key, dims, split, -0.22, 0.18) * values
    return jnp.clip(values, min=-reach, max=reach).astype(held_as)


def noise_with(key, extent, deviation, bound, cuts, heavy, kind=jnp.bfloat16):
    array = deviation * jax.random.normal(key, extent, jnp.float32)
    if cuts:
        array = array * block_levels(key, extent, cuts, -0.22, 0.18)
    return jnp.clip(spiked(array, jax.random.fold_in(key, 3), *heavy), -bound, bound).astype(kind)


def setup_inputs(seed: int = 0, part: int = 0) -> dict:
    streams_of = jax.random.split(jax.random.key(seed), 5)
    own_keys = jax.random.split(jax.random.fold_in(streams_of[4], part), 5)
    return {
        "library": noise_with(own_keys[0], (SUBFAULTS, GAUGES, TAPS), (TAPS * ACTIVE // 2) ** -0.5, 0.25, ((0, 4), (1, 2)), (0, 1, 4, 2.0), jnp.float32),
        "rates": noise(own_keys[1], (SCEN, ACTIVE, SAMPLES), 1.0, 6.0, ((1, 4), (2, 2)), jnp.float32),
        "subfault_ids": draw_subfault_ids(jax.random.fold_in(jax.random.fold_in(streams_of[4], part), 71), part),
        "onsets": place_ends(jax.random.randint(own_keys[3], (SCEN, ACTIVE), 0, SAMPLES), jax.random.fold_in(own_keys[3], 1), 0, SAMPLES - 1).astype(jnp.int32),
    }


def reference(library, rates, subfault_ids, onsets):
    length = 2 * SAMPLES
    sample_times = jnp.arange(SAMPLES, dtype=jnp.int32)

    def one_scenario(scenario_args):
        rate_rows, id_row, onset_row = scenario_args
        masked = jnp.where(sample_times[None, :] >= onset_row[:, None], rate_rows, jnp.zeros_like(rate_rows))
        green_rows = library[id_row]
        rate_spectra = jnp.fft.rfft(masked, n=length, axis=-1)
        green_spectra = jnp.fft.rfft(green_rows, n=length, axis=-1)
        total = jnp.sum(green_spectra * rate_spectra[:, None, :], axis=0)
        return jnp.fft.irfft(total, n=length, axis=-1)[:, :SAMPLES]

    waves = lax.map(one_scenario, (rates, subfault_ids, onsets))
    return jnp.transpose(waves, (1, 0, 2)).astype(jnp.float32)
```

```python
import functools

import jax
import jax.numpy as jnp
from jax import lax
from jax.experimental import pallas as pl
from jax.experimental.pallas import tpu as pltpu
from jax.sharding import PartitionSpec as P

MESH = pl.DeviceIdType.MESH


def synth_kernel(
    sub_n, tm_n, lib_hbm, rates, ids, onsets, out,
    lib, cur, prior, ids_s, ons_s, toe_hi, toe_lo, green, part, recv,
    lib_sem, own_sem, cur_send, cur_recv, prior_send, prior_recv, wave_send, wave_recv,
):
    me = lax.axis_index("sub")
    core = lax.axis_index("tm")
    scen_n, edev, span = rates.shape
    faults, panel, taps = lib.shape
    rows = panel // sub_n
    half = taps // 2

    lib_copy = pltpu.make_async_copy(lib_hbm, lib, lib_sem)
    lib_copy.start()
    own = [
        pltpu.make_async_copy(rates, cur.at[me], own_sem.at[0]),
        pltpu.make_async_copy(ids, ids_s.at[me], own_sem.at[1]),
        pltpu.make_async_copy(onsets, ons_s.at[me], own_sem.at[2]),
    ]
    for c in own:
        c.start()
    prior[...] = jnp.zeros_like(prior)

    barrier = pltpu.get_barrier_semaphore()

    def peer(o):
        return lax.rem(me + o, sub_n)

    for o in range(1, sub_n):
        pl.semaphore_signal(barrier, inc=1, device_id={"sub": peer(o)}, device_id_type=MESH)
    for step in (-1, 1):
        @pl.when((core + step >= 0) & (core + step < tm_n))
        def _():
            for o in range(sub_n):
                pl.semaphore_signal(
                    barrier, inc=1, device_id={"sub": peer(o), "tm": core + step}, device_id_type=MESH
                )
    ends = jnp.where(core > 0, sub_n, 0) + jnp.where(core < tm_n - 1, sub_n, 0)
    pl.semaphore_wait(barrier, sub_n - 1 + ends)

    def same_tm(o):
        who = {"sub": peer(o)}
        return [
            pltpu.make_async_remote_copy(
                src_ref=src, dst_ref=dst.at[me], send_sem=cur_send.at[i, o - 1],
                recv_sem=cur_recv.at[i, o - 1], device_id=who, device_id_type=MESH,
            )
            for i, (src, dst) in enumerate(((ids, ids_s), (onsets, ons_s), (rates, cur)))
        ]

    def next_tm(o):
        return pltpu.make_async_remote_copy(
            src_ref=rates, dst_ref=prior.at[me], send_sem=prior_send.at[o],
            recv_sem=prior_recv.at[o], device_id={"sub": peer(o), "tm": core + 1}, device_id_type=MESH,
        )

    def from_tm(o):
        return pltpu.make_async_remote_copy(
            src_ref=rates, dst_ref=prior.at[lax.rem(me - o + sub_n, sub_n)], send_sem=prior_send.at[o],
            recv_sem=prior_recv.at[o], device_id={"sub": peer(o), "tm": core}, device_id_type=MESH,
        )

    def from_same(o):
        src_dev = lax.rem(me - o + sub_n, sub_n)
        return [
            pltpu.make_async_remote_copy(
                src_ref=src, dst_ref=dst.at[src_dev], send_sem=cur_send.at[i, o - 1],
                recv_sem=cur_recv.at[i, o - 1], device_id={"sub": peer(o)}, device_id_type=MESH,
            )
            for i, (src, dst) in enumerate(((ids, ids_s), (onsets, ons_s), (rates, cur)))
        ]

    for o in range(sub_n - 1, 0, -1):
        for c in same_tm(o):
            c.start()

    @pl.when(core < tm_n - 1)
    def _():
        for o in range(sub_n - 1, -1, -1):
            next_tm(o).start()

    for c in own:
        c.wait()
    for o in range(1, sub_n):
        for c in from_same(o):
            c.wait_recv()

    @pl.when(core > 0)
    def _():
        for o in range(sub_n):
            from_tm(o).wait_recv()

    lib_copy.wait()

    times = lax.broadcasted_iota(jnp.int32, (1, 2 * span), 1) + (core - 1) * span

    def toeplitz(z, s, e, slot):
        name = ids_s[z, s, e]
        mine = (name // faults) == me
        first = jnp.where(mine, ons_s[z, s, e], jnp.int32(2**30))
        record = jnp.concatenate(
            [prior[z, s, pl.ds(e, 1), :], cur[z, s, pl.ds(e, 1), :]], axis=1
        )
        record = jnp.where(times >= first, record, 0.0)
        skewed = pltpu.roll(
            jnp.broadcast_to(record, (8, 2 * span)), 0, 1, stride=1, stride_axis=0
        )
        for pair in range(half // 16):
            two = [
                (pltpu.roll(skewed, 16 * pair + 8 * h, 1) if pair + h else skewed)[:, half:]
                for h in range(2)
            ]
            both = jnp.concatenate(two, axis=0)
            high = both.astype(jnp.bfloat16)
            toe_hi[slot, pl.ds(16 * pair, 16), :] = high
            toe_lo[slot, pl.ds(16 * pair, 16), :] = (both - high.astype(jnp.float32)).astype(jnp.bfloat16)
        where = jnp.clip(name - me * faults, 0, faults - 1)
        function = lib[where]
        high = function.astype(jnp.bfloat16)
        green[pl.ds(0, panel), pl.ds(slot * taps, taps)] = high
        green[pl.ds(panel, panel), pl.ds(slot * taps, taps)] = (
            function - high.astype(jnp.float32)
        ).astype(jnp.bfloat16)

    group = max(u for u in range(1, 5) if sub_n % u == 0)
    slots = group * edev

    def stacked(toe):
        pieces = []
        for slot in range(slots):
            pieces.append(toe[slot, :, pl.ds(half, span)])
            pieces.append(toe[slot, :, pl.ds(0, span)])
        return jnp.concatenate(pieces, axis=0)

    def wave_copy(s, o, dest, sent):
        return pltpu.make_async_remote_copy(
            src_ref=part.at[s, dest],
            dst_ref=recv.at[o - 1, s], send_sem=wave_send.at[o - 1], recv_sem=wave_recv.at[o - 1],
            device_id={"sub": dest}, device_id_type=MESH,
        )

    def scenario(s, carry):
        def block_group(first_z):
            for i in range(group):
                for e in range(edev):
                    toeplitz(first_z + i, s, e, i * edev + e)
            big = jnp.dot(green[...], stacked(toe_hi), preferred_element_type=jnp.float32)
            small = jnp.dot(green[pl.ds(0, panel), :], stacked(toe_lo), preferred_element_type=jnp.float32)
            return big[:panel] + (big[panel:] + small)

        def panels(wave):
            return [wave[rows * d : rows * (d + 1)] for d in range(sub_n)]

        for d, piece in enumerate(panels(block_group(0))):
            part[s, d] = piece
        if sub_n > group:
            def more(i, c):
                for d, piece in enumerate(panels(block_group(i * group))):
                    part[s, d] += piece
                return c
            lax.fori_loop(1, sub_n // group, more, 0)
        for o in range(sub_n - 1, 0, -1):
            wave_copy(s, o, peer(o), True).start()
        return carry

    lax.fori_loop(0, scen_n, scenario, 0)

    def whole_wave(o):
        return pltpu.make_async_remote_copy(
            src_ref=recv.at[o - 1], dst_ref=recv.at[o - 1], send_sem=wave_send.at[o - 1],
            recv_sem=wave_recv.at[o - 1], device_id={"sub": peer(o)}, device_id_type=MESH,
        )

    total = part[:, me]
    for o in range(1, sub_n):
        whole_wave(o).wait_recv()
    for o in range(1, sub_n):
        total = total + recv[o - 1]
    out[...] = total
    for o in range(1, sub_n):
        whole_wave(o).wait_send()
        for c in same_tm(o):
            c.wait_send()

    @pl.when(core < tm_n - 1)
    def _():
        for o in range(sub_n):
            next_tm(o).wait_send()


def solution(mesh):
    sub_n, tm_n = mesh.shape["sub"], mesh.shape["tm"]

    def on_device(library, rates, subfault_ids, onsets):
        faults, panel, taps = library.shape
        scen_n, edev, span = rates.shape
        rows = panel // sub_n
        group = max(u for u in range(1, 5) if sub_n % u == 0)
        slots = group * edev
        dma = pltpu.SemaphoreType.DMA
        waves = pl.pallas_call(
            functools.partial(synth_kernel, sub_n, tm_n),
            out_shape=jax.ShapeDtypeStruct((scen_n, rows, span), jnp.float32),
            in_specs=[pl.BlockSpec(memory_space=pl.ANY)] * 4,
            out_specs=pl.BlockSpec(memory_space=pltpu.VMEM),
            scratch_shapes=[
                pltpu.VMEM((faults, panel, taps), jnp.float32),
                pltpu.VMEM((sub_n, scen_n, edev, span), jnp.float32),
                pltpu.VMEM((sub_n, scen_n, edev, span), jnp.float32),
                pltpu.SMEM((sub_n, scen_n, edev), jnp.int32),
                pltpu.SMEM((sub_n, scen_n, edev), jnp.int32),
                pltpu.VMEM((slots, taps // 2, span + taps // 2), jnp.bfloat16),
                pltpu.VMEM((slots, taps // 2, span + taps // 2), jnp.bfloat16),
                pltpu.VMEM((2 * panel, slots * taps), jnp.bfloat16),
                pltpu.VMEM((scen_n, sub_n, rows, span), jnp.float32),
                pltpu.VMEM((sub_n - 1, scen_n, rows, span), jnp.float32),
                dma, dma((3,)), dma((3, sub_n - 1)), dma((3, sub_n - 1)),
                dma((sub_n,)), dma((sub_n,)), dma((sub_n - 1,)), dma((sub_n - 1,)),
            ],
            compiler_params=pltpu.CompilerParams(collective_id=0, has_side_effects=True),
        )(library, rates, subfault_ids, onsets)
        return jnp.transpose(waves, (1, 0, 2))

    in_specs = (
        P(("groups", "sub"), "gauge", None),
        P("groups", "sub", "tm"),
        P("groups", "sub"),
        P("groups", "sub"),
    )
    out_specs = P(("gauge", "sub"), "groups", "tm")
    return jax.shard_map(
        on_device, mesh=mesh, in_specs=in_specs, out_specs=out_specs, check_vma=False
    )
```

```python
import functools

import jax
import jax.numpy as jnp
from jax import lax
from jax.experimental import pallas as pl
from jax.experimental.pallas import tpu as pltpu
from jax.sharding import PartitionSpec as P

MESH = pl.DeviceIdType.MESH


def synth_kernel(
    sub_n, tm_n, lib_hbm, rates, ids, onsets, out,
    lib, cur, prior, ids_s, ons_s, toe_hi, toe_lo, green, part, recv,
    lib_sem, own_sem, cur_send, cur_recv, prior_send, prior_recv, wave_send, wave_recv,
):
    me = lax.axis_index("sub")
    core = lax.axis_index("tm")
    scen_n, edev, span = rates.shape
    faults, panel, taps = lib.shape
    rows = panel // sub_n
    half = taps // 2

    lib_copy = pltpu.make_async_copy(lib_hbm, lib, lib_sem)
    lib_copy.start()
    own = [
        pltpu.make_async_copy(rates, cur.at[me], own_sem.at[0]),
        pltpu.make_async_copy(ids, ids_s.at[me], own_sem.at[1]),
        pltpu.make_async_copy(onsets, ons_s.at[me], own_sem.at[2]),
    ]
    for c in own:
        c.start()
    prior[...] = jnp.zeros_like(prior)

    barrier = pltpu.get_barrier_semaphore()

    def peer(o):
        return lax.rem(me + o, sub_n)

    for o in range(1, sub_n):
        pl.semaphore_signal(barrier, inc=1, device_id={"sub": peer(o)}, device_id_type=MESH)
    for step in (-1, 1):
        @pl.when((core + step >= 0) & (core + step < tm_n))
        def _():
            for o in range(sub_n):
                pl.semaphore_signal(
                    barrier, inc=1, device_id={"sub": peer(o), "tm": core + step}, device_id_type=MESH
                )
    ends = jnp.where(core > 0, sub_n, 0) + jnp.where(core < tm_n - 1, sub_n, 0)
    pl.semaphore_wait(barrier, sub_n - 1 + ends)

    def same_tm(o):
        who = {"sub": peer(o)}
        return [
            pltpu.make_async_remote_copy(
                src_ref=src, dst_ref=dst.at[me], send_sem=cur_send.at[i, o - 1],
                recv_sem=cur_recv.at[i, o - 1], device_id=who, device_id_type=MESH,
            )
            for i, (src, dst) in enumerate(((ids, ids_s), (onsets, ons_s), (rates, cur)))
        ]

    def next_tm(o):
        return pltpu.make_async_remote_copy(
            src_ref=rates, dst_ref=prior.at[me], send_sem=prior_send.at[o],
            recv_sem=prior_recv.at[o], device_id={"sub": peer(o), "tm": core + 1}, device_id_type=MESH,
        )

    def from_tm(o):
        return pltpu.make_async_remote_copy(
            src_ref=rates, dst_ref=prior.at[lax.rem(me - o + sub_n, sub_n)], send_sem=prior_send.at[o],
            recv_sem=prior_recv.at[o], device_id={"sub": peer(o), "tm": core}, device_id_type=MESH,
        )

    def from_same(o):
        src_dev = lax.rem(me - o + sub_n, sub_n)
        return [
            pltpu.make_async_remote_copy(
                src_ref=src, dst_ref=dst.at[src_dev], send_sem=cur_send.at[i, o - 1],
                recv_sem=cur_recv.at[i, o - 1], device_id={"sub": peer(o)}, device_id_type=MESH,
            )
            for i, (src, dst) in enumerate(((ids, ids_s), (onsets, ons_s), (rates, cur)))
        ]

    for o in range(sub_n - 1, 0, -1):
        for c in same_tm(o):
            c.start()

    @pl.when(core < tm_n - 1)
    def _():
        for o in range(sub_n - 1, -1, -1):
            next_tm(o).start()

    for c in own:
        c.wait()
    for o in range(1, sub_n):
        for c in from_same(o):
            c.wait_recv()

    @pl.when(core > 0)
    def _():
        for o in range(sub_n):
            from_tm(o).wait_recv()

    lib_copy.wait()

    times = lax.broadcasted_iota(jnp.int32, (1, 2 * span), 1) + (core - 1) * span

    def toeplitz(z, s, e, slot):
        name = ids_s[z, e, s]
        mine = (name // faults) == me
        first = jnp.where(mine, ons_s[z, e, s], jnp.int32(2**30))
        record = jnp.concatenate(
            [prior[z, s, pl.ds(e, 1), :], cur[z, s, pl.ds(e, 1), :]], axis=1
        )
        record = jnp.where(times >= first, record, 0.0)
        skewed = pltpu.roll(
            jnp.broadcast_to(record, (8, 2 * span)), 0, 1, stride=1, stride_axis=0
        )
        for pair in range(half // 16):
            two = [
                (pltpu.roll(skewed, 16 * pair + 8 * h, 1) if pair + h else skewed)[:, half:]
                for h in range(2)
            ]
            both = jnp.concatenate(two, axis=0)
            high = both.astype(jnp.bfloat16)
            toe_hi[slot, pl.ds(16 * pair, 16), :] = high
            toe_lo[slot, pl.ds(16 * pair, 16), :] = (both - high.astype(jnp.float32)).astype(jnp.bfloat16)
        where = jnp.clip(name - me * faults, 0, faults - 1)
        function = lib[where]
        high = function.astype(jnp.bfloat16)
        green[pl.ds(0, panel), pl.ds(slot * taps, taps)] = high
        green[pl.ds(panel, panel), pl.ds(slot * taps, taps)] = (
            function - high.astype(jnp.float32)
        ).astype(jnp.bfloat16)

    group = max(u for u in range(1, 5) if sub_n % u == 0)
    slots = group * edev

    def stacked(toe):
        pieces = []
        for slot in range(slots):
            pieces.append(toe[slot, :, pl.ds(half, span)])
            pieces.append(toe[slot, :, pl.ds(0, span)])
        return jnp.concatenate(pieces, axis=0)

    def wave_copy(s, o, dest, sent):
        return pltpu.make_async_remote_copy(
            src_ref=part.at[s, dest],
            dst_ref=recv.at[o - 1, s], send_sem=wave_send.at[o - 1], recv_sem=wave_recv.at[o - 1],
            device_id={"sub": dest}, device_id_type=MESH,
        )

    def scenario(s, carry):
        def block_group(first_z):
            for i in range(group):
                for e in range(edev):
                    toeplitz(first_z + i, s, e, i * edev + e)
            big = jnp.dot(green[...], stacked(toe_hi), preferred_element_type=jnp.float32)
            small = jnp.dot(green[pl.ds(0, panel), :], stacked(toe_lo), preferred_element_type=jnp.float32)
            return big[:panel] + (big[panel:] + small)

        def panels(wave):
            return [wave[rows * d : rows * (d + 1)] for d in range(sub_n)]

        for d, piece in enumerate(panels(block_group(0))):
            part[s, d] = piece
        if sub_n > group:
            def more(i, c):
                for d, piece in enumerate(panels(block_group(i * group))):
                    part[s, d] += piece
                return c
            lax.fori_loop(1, sub_n // group, more, 0)
        for o in range(sub_n - 1, 0, -1):
            wave_copy(s, o, peer(o), True).start()
        return carry

    lax.fori_loop(0, scen_n, scenario, 0)

    def whole_wave(o):
        return pltpu.make_async_remote_copy(
            src_ref=recv.at[o - 1], dst_ref=recv.at[o - 1], send_sem=wave_send.at[o - 1],
            recv_sem=wave_recv.at[o - 1], device_id={"sub": peer(o)}, device_id_type=MESH,
        )

    total = part[:, me]
    for o in range(1, sub_n):
        whole_wave(o).wait_recv()
    for o in range(1, sub_n):
        total = total + recv[o - 1]
    out[...] = jnp.swapaxes(total, 0, 1)
    for o in range(1, sub_n):
        whole_wave(o).wait_send()
        for c in same_tm(o):
            c.wait_send()

    @pl.when(core < tm_n - 1)
    def _():
        for o in range(sub_n):
            next_tm(o).wait_send()


def solution(mesh):
    sub_n, tm_n = mesh.shape["sub"], mesh.shape["tm"]

    def on_device(library, rates, subfault_ids, onsets):
        faults, panel, taps = library.shape
        scen_n, edev, span = rates.shape
        rows = panel // sub_n
        group = max(u for u in range(1, 5) if sub_n % u == 0)
        slots = group * edev
        dma = pltpu.SemaphoreType.DMA
        waves = pl.pallas_call(
            functools.partial(synth_kernel, sub_n, tm_n),
            out_shape=jax.ShapeDtypeStruct((rows, scen_n, span), jnp.float32),
            in_specs=[pl.BlockSpec(memory_space=pl.ANY)] * 4,
            out_specs=pl.BlockSpec(memory_space=pltpu.VMEM),
            scratch_shapes=[
                pltpu.VMEM((faults, panel, taps), jnp.float32),
                pltpu.VMEM((sub_n, scen_n, edev, span), jnp.float32),
                pltpu.VMEM((sub_n, scen_n, edev, span), jnp.float32),
                pltpu.SMEM((sub_n, edev, scen_n), jnp.int32),
                pltpu.SMEM((sub_n, edev, scen_n), jnp.int32),
                pltpu.VMEM((slots, taps // 2, span + taps // 2), jnp.bfloat16),
                pltpu.VMEM((slots, taps // 2, span + taps // 2), jnp.bfloat16),
                pltpu.VMEM((2 * panel, slots * taps), jnp.bfloat16),
                pltpu.VMEM((scen_n, sub_n, rows, span), jnp.float32),
                pltpu.VMEM((sub_n - 1, scen_n, rows, span), jnp.float32),
                dma, dma((3,)), dma((3, sub_n - 1)), dma((3, sub_n - 1)),
                dma((sub_n,)), dma((sub_n,)), dma((sub_n - 1,)), dma((sub_n - 1,)),
            ],
            compiler_params=pltpu.CompilerParams(collective_id=0, has_side_effects=True),
        )(library, rates, subfault_ids.T, onsets.T)
        return waves

    in_specs = (
        P(("groups", "sub"), "gauge", None),
        P("groups", "sub", "tm"),
        P("groups", "sub"),
        P("groups", "sub"),
    )
    out_specs = P(("gauge", "sub"), "groups", "tm")
    return jax.shard_map(
        on_device, mesh=mesh, in_specs=in_specs, out_specs=out_specs, check_vma=False
    )
```

```python
import functools

import jax
import jax.numpy as jnp
from jax import lax
from jax.experimental import pallas as pl
from jax.experimental.pallas import tpu as pltpu
from jax.sharding import PartitionSpec as P

MESH = pl.DeviceIdType.MESH


def synth_kernel(
    sub_n, tm_n, lib_hbm, rates, ids, onsets, out,
    lib, cur, prior, ids_s, ons_s, toe_hi, toe_lo, green, skew, turns, part, direct, lent, joint, recv,
    lib_sem, own_sem, cur_send, cur_recv, prior_send, prior_recv,
    direct_sem, lend_send, lend_recv, wave_send, wave_recv,
):
    me = lax.axis_index("sub")
    core = lax.axis_index("tm")
    scen_n, edev, span = rates.shape
    faults, panel, taps = lib.shape
    rows = panel // sub_n
    half = taps // 2
    group = max(u for u in range(1, 5) if sub_n % u == 0)
    slots = group * edev
    rolled = half // 16 - turns.shape[0]

    lib_copy = pltpu.make_async_copy(lib_hbm, lib, lib_sem)
    lib_copy.start()
    own = [
        pltpu.make_async_copy(rates, cur.at[me], own_sem.at[0]),
        pltpu.make_async_copy(ids, ids_s.at[me], own_sem.at[1]),
        pltpu.make_async_copy(onsets, ons_s.at[me], own_sem.at[2]),
    ]
    for c in own:
        c.start()
    prior[...] = jnp.zeros_like(prior)

    barrier = pltpu.get_barrier_semaphore()

    def peer(o):
        return lax.rem(me + o, sub_n)

    for o in range(1, sub_n):
        pl.semaphore_signal(barrier, inc=1, device_id={"sub": peer(o)}, device_id_type=MESH)
    for step in (-1, 1):
        @pl.when((core + step >= 0) & (core + step < tm_n))
        def _():
            for o in range(sub_n):
                pl.semaphore_signal(
                    barrier, inc=1, device_id={"sub": peer(o), "tm": core + step}, device_id_type=MESH
                )
    ends = jnp.where(core > 0, sub_n, 0) + jnp.where(core < tm_n - 1, sub_n, 0)
    pl.semaphore_wait(barrier, sub_n - 1 + ends)

    def same_tm(o):
        who = {"sub": peer(o)}
        return [
            pltpu.make_async_remote_copy(
                src_ref=src, dst_ref=dst.at[me], send_sem=cur_send.at[i, o - 1],
                recv_sem=cur_recv.at[i, o - 1], device_id=who, device_id_type=MESH,
            )
            for i, (src, dst) in enumerate(((ids, ids_s), (onsets, ons_s), (rates, cur)))
        ]

    def next_tm(o):
        return pltpu.make_async_remote_copy(
            src_ref=rates, dst_ref=prior.at[me], send_sem=prior_send.at[o],
            recv_sem=prior_recv.at[o], device_id={"sub": peer(o), "tm": core + 1}, device_id_type=MESH,
        )

    def from_tm(o):
        return pltpu.make_async_remote_copy(
            src_ref=rates, dst_ref=prior.at[lax.rem(me - o + sub_n, sub_n)], send_sem=prior_send.at[o],
            recv_sem=prior_recv.at[o], device_id={"sub": peer(o), "tm": core}, device_id_type=MESH,
        )

    def from_same(o):
        src_dev = lax.rem(me - o + sub_n, sub_n)
        return [
            pltpu.make_async_remote_copy(
                src_ref=src, dst_ref=dst.at[src_dev], send_sem=cur_send.at[i, o - 1],
                recv_sem=cur_recv.at[i, o - 1], device_id={"sub": peer(o)}, device_id_type=MESH,
            )
            for i, (src, dst) in enumerate(((ids, ids_s), (onsets, ons_s), (rates, cur)))
        ]

    for o in range(sub_n - 1, 0, -1):
        for c in same_tm(o):
            c.start()

    @pl.when(core < tm_n - 1)
    def _():
        for o in range(sub_n - 1, -1, -1):
            next_tm(o).start()

    source = lax.broadcasted_iota(jnp.int32, (256, 128), 0)
    target = lax.broadcasted_iota(jnp.int32, (256, 128), 1) + 128
    for i in range(turns.shape[0]):
        for h in range(2):
            shift = 16 * (rolled + i) + 8 * h
            turns[i, :, pl.ds(128 * h, 128)] = jnp.where(source == target - shift, 1.0, 0.0).astype(jnp.bfloat16)

    for c in own:
        c.wait()
    for o in range(1, sub_n):
        for c in from_same(o):
            c.wait_recv()

    @pl.when(core > 0)
    def _():
        for o in range(sub_n):
            from_tm(o).wait_recv()

    lib_copy.wait()

    times = lax.broadcasted_iota(jnp.int32, (1, 2 * span), 1) + (core - 1) * span

    def toeplitz(z, s, e, slot):
        name = ids_s[z, e, s]
        mine = (name // faults) == me
        first = jnp.where(mine, ons_s[z, e, s], jnp.int32(2**30))
        record = jnp.concatenate(
            [prior[z, s, pl.ds(e, 1), :], cur[z, s, pl.ds(e, 1), :]], axis=1
        )
        record = jnp.where(times >= first, record, 0.0)
        skewed = pltpu.roll(
            jnp.broadcast_to(record, (8, 2 * span)), 0, 1, stride=1, stride_axis=0
        )
        top = skewed.astype(jnp.bfloat16).astype(jnp.float32)
        skew[pl.ds(8 * slot, 8), :] = top
        skew[pl.ds(8 * (slots + slot), 8), :] = skewed - top
        for pair in range(rolled):
            two = [
                (pltpu.roll(skewed, 16 * pair + 8 * h, 1) if pair + h else skewed)[:, half:]
                for h in range(2)
            ]
            both = jnp.concatenate(two, axis=0)
            high = both.astype(jnp.bfloat16)
            toe_hi[slot, pl.ds(16 * pair, 16), :] = high
            toe_lo[slot, pl.ds(16 * pair, 16), :] = (both - high.astype(jnp.float32)).astype(jnp.bfloat16)
        where = jnp.clip(name - me * faults, 0, faults - 1)
        function = lib[where]
        high = function.astype(jnp.bfloat16)
        green[pl.ds(0, panel), pl.ds(slot * taps, taps)] = high
        green[pl.ds(panel, panel), pl.ds(slot * taps, taps)] = (
            function - high.astype(jnp.float32)
        ).astype(jnp.bfloat16)

    def turned():
        steps = half // 128 + span // 128
        wide = jnp.concatenate(
            [skew[:, pl.ds(128 * v, 256)] for v in range(steps)], axis=0
        ).astype(jnp.bfloat16)
        for pair in range(rolled, half // 16):
            moved = jnp.dot(wide, turns[pair - rolled], preferred_element_type=jnp.float32)
            for v in range(steps):
                for h, toe in enumerate((toe_hi, toe_lo)):
                    for slot in range(slots):
                        row = 16 * slots * v + 8 * (slots * h + slot)
                        piece = moved[row : row + 8]
                        toe[slot, pl.ds(16 * pair, 16), pl.ds(128 * v, 128)] = jnp.concatenate(
                            [piece[:, :128], piece[:, 128:]], axis=0
                        ).astype(jnp.bfloat16)

    def stacked(toe):
        pieces = []
        for slot in range(slots):
            pieces.append(toe[slot, :, pl.ds(half, span)])
            pieces.append(toe[slot, :, pl.ds(0, span)])
        return jnp.concatenate(pieces, axis=0)

    right = lax.rem(me, 2)
    pair, pairs = me // 2, sub_n // 2
    mate = me + 1 - 2 * right

    def far_pair(o):
        return lax.rem(pair + o, pairs)

    def outer(o):
        return jnp.where(far_pair(o) > pair, 1 - right, right) == 1

    def remote(src, dst, send, recv_at, dest):
        return pltpu.make_async_remote_copy(
            src_ref=src, dst_ref=dst, send_sem=send, recv_sem=recv_at,
            device_id={"sub": dest}, device_id_type=MESH,
        )

    def to_mate(s):
        return remote(part.at[s, mate], direct.at[s], direct_sem.at[0], direct_sem.at[1], mate)

    def lend(s, o):
        return remote(
            part.at[s, pl.ds(2 * far_pair(o), 2)], lent.at[o - 1, s],
            lend_send.at[o - 1], lend_recv.at[o - 1, s], mate,
        )

    def deliver(s, o, j):
        return remote(
            joint.at[o - 1, s, j], recv.at[o - 1, s],
            wave_send.at[o - 1], wave_recv.at[o - 1], 2 * far_pair(o) + j,
        )

    def forward(s):
        for o in range(1, pairs):
            @pl.when(jnp.logical_not(outer(o)))
            def _():
                lend(s, o).wait_recv()
                joint[o - 1, s] = part[s, pl.ds(2 * far_pair(o), 2)] + lent[o - 1, s]
                deliver(s, o, 0).start()
                deliver(s, o, 1).start()

    lag = 2

    def scenario(s, carry):
        def block_group(first_z):
            for i in range(group):
                for e in range(edev):
                    toeplitz(first_z + i, s, e, i * edev + e)
            turned()
            big = jnp.dot(green[...], stacked(toe_hi), preferred_element_type=jnp.float32)
            small = jnp.dot(green[pl.ds(0, panel), :], stacked(toe_lo), preferred_element_type=jnp.float32)
            return big[:panel] + (big[panel:] + small)

        def panels(wave):
            return [wave[rows * d : rows * (d + 1)] for d in range(sub_n)]

        for d, piece in enumerate(panels(block_group(0))):
            part[s, d] = piece
        if sub_n > group:
            def more(i, c):
                for d, piece in enumerate(panels(block_group(i * group))):
                    part[s, d] += piece
                return c
            lax.fori_loop(1, sub_n // group, more, 0)
        for o in range(1, pairs):
            @pl.when(outer(o))
            def _():
                lend(s, o).start()
        to_mate(s).start()

        @pl.when(s >= lag)
        def _():
            forward(s - lag)
        return carry

    lax.fori_loop(0, scen_n, scenario, 0)

    def rest(s, carry):
        forward(s)
        return carry

    lax.fori_loop(scen_n - lag, scen_n, rest, 0)

    def whole(ref, send, recv_at):
        return remote(ref, ref, send, recv_at, mate)

    total = part[:, me]
    whole(direct, direct_sem.at[0], direct_sem.at[1]).wait_recv()
    total = total + direct[...]
    for o in range(1, pairs):
        whole(recv.at[o - 1], wave_send.at[o - 1], wave_recv.at[o - 1]).wait_recv()
    for o in range(1, pairs):
        total = total + recv[o - 1]
    out[...] = jnp.swapaxes(total, 0, 1)
    whole(direct, direct_sem.at[0], direct_sem.at[1]).wait_send()
    for o in range(1, pairs):
        @pl.when(outer(o))
        def _():
            whole(lent.at[o - 1], lend_send.at[o - 1], wave_recv.at[o - 1]).wait_send()

        @pl.when(jnp.logical_not(outer(o)))
        def _():
            whole(joint.at[o - 1], wave_send.at[o - 1], wave_recv.at[o - 1]).wait_send()
    for o in range(1, sub_n):
        for c in same_tm(o):
            c.wait_send()

    @pl.when(core < tm_n - 1)
    def _():
        for o in range(sub_n):
            next_tm(o).wait_send()


def solution(mesh):
    sub_n, tm_n = mesh.shape["sub"], mesh.shape["tm"]

    def on_device(library, rates, subfault_ids, onsets):
        faults, panel, taps = library.shape
        scen_n, edev, span = rates.shape
        rows = panel // sub_n
        group = max(u for u in range(1, 5) if sub_n % u == 0)
        slots, pairs = group * edev, sub_n // 2
        dma = pltpu.SemaphoreType.DMA
        waves = pl.pallas_call(
            functools.partial(synth_kernel, sub_n, tm_n),
            out_shape=pltpu.VMEM((rows, scen_n, span), jnp.float32),
            in_specs=[pl.BlockSpec(memory_space=pltpu.HBM)] * 4,
            out_specs=pl.BlockSpec(memory_space=pltpu.VMEM),
            scratch_shapes=[
                pltpu.VMEM((faults, panel, taps), jnp.float32),
                pltpu.VMEM((sub_n, scen_n, edev, span), jnp.float32),
                pltpu.VMEM((sub_n, scen_n, edev, span), jnp.float32),
                pltpu.SMEM((sub_n, edev, scen_n), jnp.int32),
                pltpu.SMEM((sub_n, edev, scen_n), jnp.int32),
                pltpu.VMEM((slots, taps // 2, span + taps // 2), jnp.bfloat16),
                pltpu.VMEM((slots, taps // 2, span + taps // 2), jnp.bfloat16),
                pltpu.VMEM((2 * panel, slots * taps), jnp.bfloat16),
                pltpu.VMEM((16 * slots, 2 * span), jnp.float32),
                pltpu.VMEM((taps // 32 - taps * 6 // 256, 256, 256), jnp.bfloat16),
                pltpu.VMEM((scen_n, sub_n, rows, span), jnp.float32),
                pltpu.VMEM((scen_n, rows, span), jnp.float32),
                pltpu.VMEM((pairs - 1, scen_n, 2, rows, span), jnp.float32),
                pltpu.VMEM((pairs - 1, scen_n, 2, rows, span), jnp.float32),
                pltpu.VMEM((pairs - 1, scen_n, rows, span), jnp.float32),
                dma, dma((3,)), dma((3, sub_n - 1)), dma((3, sub_n - 1)),
                dma((sub_n,)), dma((sub_n,)), dma((2,)), dma((pairs - 1,)), dma((pairs - 1, scen_n)),
                dma((pairs - 1,)), dma((pairs - 1,)),
            ],
            compiler_params=pltpu.CompilerParams(collective_id=0, has_side_effects=True, vmem_limit_bytes=40 * 2**20),
        )(*(pltpu.with_memory_space_constraint(x, pltpu.HBM) for x in (library, rates, subfault_ids.T, onsets.T)))
        return waves

    in_specs = (
        P(("groups", "sub"), "gauge", None),
        P("groups", "sub", "tm"),
        P("groups", "sub"),
        P("groups", "sub"),
    )
    out_specs = P(("gauge", "sub"), "groups", "tm")
    return jax.shard_map(
        on_device, mesh=mesh, in_specs=in_specs, out_specs=out_specs, check_vma=False
    )
```

```python
import functools

import jax
import jax.numpy as jnp
from jax import lax
from jax.experimental import pallas as pl
from jax.experimental.pallas import tpu as pltpu
from jax.sharding import PartitionSpec as P

MESH = pl.DeviceIdType.MESH


def synth_kernel(
    sub_n, tm_n, lib_hbm, rates, ids, onsets, out,
    lib, cur, prior, ids_s, ons_s, toe_hi, toe_lo, green, skew, turns, part, direct, lent, joint, recv,
    lib_sem, own_sem, cur_send, cur_recv, prior_send, prior_recv,
    direct_sem, lend_send, lend_recv, wave_send, wave_recv,
):
    me = lax.axis_index("sub")
    core = lax.axis_index("tm")
    scen_n, edev, span = rates.shape
    faults, panel, taps = lib.shape
    rows = panel // sub_n
    half = taps // 2
    group = max(u for u in range(1, 5) if sub_n % u == 0)
    slots = group * edev
    rolled = half // 16 - turns.shape[0]

    barrier = pltpu.get_barrier_semaphore()

    def peer(o):
        return lax.rem(me + o, sub_n)

    for o in range(1, sub_n):
        pl.semaphore_signal(barrier, inc=1, device_id={"sub": peer(o)}, device_id_type=MESH)
    for step in (-1, 1):
        @pl.when((core + step >= 0) & (core + step < tm_n))
        def _():
            for o in range(sub_n):
                pl.semaphore_signal(
                    barrier, inc=1, device_id={"sub": peer(o), "tm": core + step}, device_id_type=MESH
                )
    lib_copy = pltpu.make_async_copy(lib_hbm, lib, lib_sem)
    lib_copy.start()
    own = [
        pltpu.make_async_copy(rates, cur.at[me], own_sem.at[0]),
        pltpu.make_async_copy(ids, ids_s.at[me], own_sem.at[1]),
        pltpu.make_async_copy(onsets, ons_s.at[me], own_sem.at[2]),
    ]
    for c in own:
        c.start()

    @pl.when(core == 0)
    def _():
        prior[...] = jnp.zeros_like(prior)

    ends = jnp.where(core > 0, sub_n, 0) + jnp.where(core < tm_n - 1, sub_n, 0)
    pl.semaphore_wait(barrier, sub_n - 1 + ends)

    def same_tm(o):
        who = {"sub": peer(o)}
        return [
            pltpu.make_async_remote_copy(
                src_ref=src, dst_ref=dst.at[me], send_sem=cur_send.at[i, o - 1],
                recv_sem=cur_recv.at[i, o - 1], device_id=who, device_id_type=MESH,
            )
            for i, (src, dst) in enumerate(((ids, ids_s), (onsets, ons_s), (rates, cur)))
        ]

    def next_tm(o):
        return pltpu.make_async_remote_copy(
            src_ref=rates, dst_ref=prior.at[me], send_sem=prior_send.at[o],
            recv_sem=prior_recv.at[o], device_id={"sub": peer(o), "tm": core + 1}, device_id_type=MESH,
        )

    def from_tm(o):
        return pltpu.make_async_remote_copy(
            src_ref=rates, dst_ref=prior.at[lax.rem(me - o + sub_n, sub_n)], send_sem=prior_send.at[o],
            recv_sem=prior_recv.at[o], device_id={"sub": peer(o), "tm": core}, device_id_type=MESH,
        )

    def from_same(o):
        src_dev = lax.rem(me - o + sub_n, sub_n)
        return [
            pltpu.make_async_remote_copy(
                src_ref=src, dst_ref=dst.at[src_dev], send_sem=cur_send.at[i, o - 1],
                recv_sem=cur_recv.at[i, o - 1], device_id={"sub": peer(o)}, device_id_type=MESH,
            )
            for i, (src, dst) in enumerate(((ids, ids_s), (onsets, ons_s), (rates, cur)))
        ]

    for o in range(sub_n - 1, 0, -1):
        for c in same_tm(o):
            c.start()

    @pl.when(core < tm_n - 1)
    def _():
        for o in range(sub_n - 1, -1, -1):
            next_tm(o).start()

    source = lax.broadcasted_iota(jnp.int32, (256, 128), 0)
    target = lax.broadcasted_iota(jnp.int32, (256, 128), 1) + 128
    for i in range(turns.shape[0]):
        for h in range(2):
            shift = 16 * (rolled + i) + 8 * h
            turns[i, :, pl.ds(128 * h, 128)] = jnp.where(source == target - shift, 1.0, 0.0).astype(jnp.bfloat16)

    for c in own:
        c.wait()
    for o in range(1, sub_n):
        for c in from_same(o):
            c.wait_recv()

    @pl.when(core > 0)
    def _():
        for o in range(sub_n):
            from_tm(o).wait_recv()

    lib_copy.wait()

    times = lax.broadcasted_iota(jnp.int32, (1, 2 * span), 1) + (core - 1) * span

    def toeplitz(z, s, e, slot):
        name = ids_s[z, e, s]
        mine = (name // faults) == me
        first = jnp.where(mine, ons_s[z, e, s], jnp.int32(2**30))
        record = jnp.concatenate(
            [prior[z, s, pl.ds(e, 1), :], cur[z, s, pl.ds(e, 1), :]], axis=1
        )
        record = jnp.where(times >= first, record, 0.0)
        skewed = pltpu.roll(
            jnp.broadcast_to(record, (8, 2 * span)), 0, 1, stride=1, stride_axis=0
        )
        top = skewed.astype(jnp.bfloat16).astype(jnp.float32)
        skew[pl.ds(8 * slot, 8), :] = top
        skew[pl.ds(8 * (slots + slot), 8), :] = skewed - top
        for pair in range(rolled):
            two = [
                (pltpu.roll(skewed, 16 * pair + 8 * h, 1) if pair + h else skewed)[:, half:]
                for h in range(2)
            ]
            both = jnp.concatenate(two, axis=0)
            high = both.astype(jnp.bfloat16)
            toe_hi[slot, pl.ds(16 * pair, 16), :] = high
            toe_lo[slot, pl.ds(16 * pair, 16), :] = (both - high.astype(jnp.float32)).astype(jnp.bfloat16)
        where = jnp.clip(name - me * faults, 0, faults - 1)
        function = lib[where]
        high = function.astype(jnp.bfloat16)
        green[pl.ds(0, panel), pl.ds(slot * taps, taps)] = high
        green[pl.ds(panel, panel), pl.ds(slot * taps, taps)] = (
            function - high.astype(jnp.float32)
        ).astype(jnp.bfloat16)

    def turned():
        steps = half // 128 + span // 128
        wide = jnp.concatenate(
            [skew[:, pl.ds(128 * v, 256)] for v in range(steps)], axis=0
        ).astype(jnp.bfloat16)
        for pair in range(rolled, half // 16):
            moved = jnp.dot(wide, turns[pair - rolled], preferred_element_type=jnp.float32)
            for v in range(steps):
                for h, toe in enumerate((toe_hi, toe_lo)):
                    for slot in range(slots):
                        row = 16 * slots * v + 8 * (slots * h + slot)
                        piece = moved[row : row + 8]
                        toe[slot, pl.ds(16 * pair, 16), pl.ds(128 * v, 128)] = jnp.concatenate(
                            [piece[:, :128], piece[:, 128:]], axis=0
                        ).astype(jnp.bfloat16)

    def stacked(toe):
        pieces = []
        for slot in range(slots):
            pieces.append(toe[slot, :, pl.ds(half, span)])
            pieces.append(toe[slot, :, pl.ds(0, span)])
        return jnp.concatenate(pieces, axis=0)

    right = lax.rem(me, 2)
    pair, pairs = me // 2, sub_n // 2
    mate = me + 1 - 2 * right

    def far_pair(o):
        return lax.rem(pair + o, pairs)

    def outer(o):
        return jnp.where(far_pair(o) > pair, 1 - right, right) == 1

    def remote(src, dst, send, recv_at, dest):
        return pltpu.make_async_remote_copy(
            src_ref=src, dst_ref=dst, send_sem=send, recv_sem=recv_at,
            device_id={"sub": dest}, device_id_type=MESH,
        )

    def to_mate(s):
        return remote(part.at[s, mate], direct.at[s], direct_sem.at[0], direct_sem.at[1], mate)

    def lend(s, o):
        return remote(
            part.at[s, pl.ds(2 * far_pair(o), 2)], lent.at[o - 1, s],
            lend_send.at[o - 1], lend_recv.at[o - 1, s], mate,
        )

    def deliver(s, o, j):
        return remote(
            joint.at[o - 1, s, j], recv.at[o - 1, s],
            wave_send.at[o - 1], wave_recv.at[o - 1], 2 * far_pair(o) + j,
        )

    def forward(s):
        for o in range(1, pairs):
            @pl.when(jnp.logical_not(outer(o)))
            def _():
                lend(s, o).wait_recv()
                joint[o - 1, s] = part[s, pl.ds(2 * far_pair(o), 2)] + lent[o - 1, s]
                deliver(s, o, 0).start()
                deliver(s, o, 1).start()

    lag = 1

    def scenario(s, carry):
        def block_group(first_z):
            for i in range(group):
                for e in range(edev):
                    toeplitz(first_z + i, s, e, i * edev + e)
            turned()
            big = jnp.dot(green[...], stacked(toe_hi), preferred_element_type=jnp.float32)
            small = jnp.dot(green[pl.ds(0, panel), :], stacked(toe_lo), preferred_element_type=jnp.float32)
            return big[:panel] + (big[panel:] + small)

        def panels(wave):
            return [wave[rows * d : rows * (d + 1)] for d in range(sub_n)]

        for d, piece in enumerate(panels(block_group(0))):
            part[s, d] = piece
        if sub_n > group:
            def more(i, c):
                for d, piece in enumerate(panels(block_group(i * group))):
                    part[s, d] += piece
                return c
            lax.fori_loop(1, sub_n // group, more, 0)
        for o in range(1, pairs):
            @pl.when(outer(o))
            def _():
                lend(s, o).start()
        to_mate(s).start()

        @pl.when(s >= lag)
        def _():
            forward(s - lag)
        return carry

    lax.fori_loop(0, scen_n, scenario, 0)

    def rest(s, carry):
        forward(s)
        return carry

    lax.fori_loop(scen_n - lag, scen_n, rest, 0)

    def whole(ref, send, recv_at):
        return remote(ref, ref, send, recv_at, mate)

    total = part[:, me]
    whole(direct, direct_sem.at[0], direct_sem.at[1]).wait_recv()
    total = total + direct[...]
    for o in range(1, pairs):
        whole(recv.at[o - 1], wave_send.at[o - 1], wave_recv.at[o - 1]).wait_recv()
    for o in range(1, pairs):
        total = total + recv[o - 1]
    out[...] = jnp.swapaxes(total, 0, 1)
    whole(direct, direct_sem.at[0], direct_sem.at[1]).wait_send()
    for o in range(1, pairs):
        @pl.when(outer(o))
        def _():
            whole(lent.at[o - 1], lend_send.at[o - 1], wave_recv.at[o - 1]).wait_send()

        @pl.when(jnp.logical_not(outer(o)))
        def _():
            whole(joint.at[o - 1], wave_send.at[o - 1], wave_recv.at[o - 1]).wait_send()
    for o in range(1, sub_n):
        for c in same_tm(o):
            c.wait_send()

    @pl.when(core < tm_n - 1)
    def _():
        for o in range(sub_n):
            next_tm(o).wait_send()


def solution(mesh):
    sub_n, tm_n = mesh.shape["sub"], mesh.shape["tm"]

    def on_device(library, rates, subfault_ids, onsets):
        faults, panel, taps = library.shape
        scen_n, edev, span = rates.shape
        rows = panel // sub_n
        group = max(u for u in range(1, 5) if sub_n % u == 0)
        slots, pairs = group * edev, sub_n // 2
        dma = pltpu.SemaphoreType.DMA
        waves = pl.pallas_call(
            functools.partial(synth_kernel, sub_n, tm_n),
            out_shape=pltpu.VMEM((rows, scen_n, span), jnp.float32),
            in_specs=[pl.BlockSpec(memory_space=pltpu.HBM)] * 4,
            out_specs=pl.BlockSpec(memory_space=pltpu.VMEM),
            scratch_shapes=[
                pltpu.VMEM((faults, panel, taps), jnp.float32),
                pltpu.VMEM((sub_n, scen_n, edev, span), jnp.float32),
                pltpu.VMEM((sub_n, scen_n, edev, span), jnp.float32),
                pltpu.SMEM((sub_n, edev, scen_n), jnp.int32),
                pltpu.SMEM((sub_n, edev, scen_n), jnp.int32),
                pltpu.VMEM((slots, taps // 2, span + taps // 2), jnp.bfloat16),
                pltpu.VMEM((slots, taps // 2, span + taps // 2), jnp.bfloat16),
                pltpu.VMEM((2 * panel, slots * taps), jnp.bfloat16),
                pltpu.VMEM((16 * slots, 2 * span), jnp.float32),
                pltpu.VMEM((taps // 32 - taps * 6 // 256, 256, 256), jnp.bfloat16),
                pltpu.VMEM((scen_n, sub_n, rows, span), jnp.float32),
                pltpu.VMEM((scen_n, rows, span), jnp.float32),
                pltpu.VMEM((pairs - 1, scen_n, 2, rows, span), jnp.float32),
                pltpu.VMEM((pairs - 1, scen_n, 2, rows, span), jnp.float32),
                pltpu.VMEM((pairs - 1, scen_n, rows, span), jnp.float32),
                dma, dma((3,)), dma((3, sub_n - 1)), dma((3, sub_n - 1)),
                dma((sub_n,)), dma((sub_n,)), dma((2,)), dma((pairs - 1,)), dma((pairs - 1, scen_n)),
                dma((pairs - 1,)), dma((pairs - 1,)),
            ],
            compiler_params=pltpu.CompilerParams(collective_id=0, has_side_effects=True, vmem_limit_bytes=40 * 2**20),
        )(*(pltpu.with_memory_space_constraint(x, pltpu.HBM) for x in (library, rates, subfault_ids.T, onsets.T)))
        return waves

    in_specs = (
        P(("groups", "sub"), "gauge", None),
        P("groups", "sub", "tm"),
        P("groups", "sub"),
        P("groups", "sub"),
    )
    out_specs = P(("gauge", "sub"), "groups", "tm")
    return jax.shard_map(
        on_device, mesh=mesh, in_specs=in_specs, out_specs=out_specs, check_vma=False
    )
```
